32 devices in a mesh: parts: 2 (over x), seq: 16 (over z, y, core).
Axes of the slice: x: 2, y: 2, z: 4, core: 2. Of those that a mesh axis runs over, the one named last changes fastest.
Arguments:
- conv_input: bfloat16 [32768, 2816], P(('parts', 'seq')), parts along dimension 0, may hold values from -6 to 6
- step_raw: bfloat16 [32768, 40], P(('parts', 'seq')), parts along dimension 0, may hold values from -4 to 4
- conv_weight: float32 [4, 2816], replicated, may hold values from -3 to 3
- conv_bias: float32 [2816], replicated, may hold values from -3 to 3
- step_bias: float32 [40], replicated, may hold values from -1 to 1
- decay_rate: float32 [40], replicated, may hold values from 1.8310547e-07 to 0.05, as said below
- norm_gain: float32 [2560], replicated, may hold values from 0.1 to 1.9
Outputs:
- layer_out: bfloat16 [32768, 2560], P(('parts', 'seq')), parts along dimension 0
The draws below stay inside these ranges and needn't reach their ends.
There are 2 independent parts, one for each index of `parts`. The reference program is written for one: setup_inputs(seed, part) draws one part's arguments, and reference() takes and returns one part's arrays. A program takes and returns all parts, laid end to end along the dimension named above; an argument that names none is the same for every part. Nothing has to cross between parts.
Inputs may be any that keep to these rules, and one draw needn't show every extreme that they name: `decay_rate`: positive decay rates, one per head.
All inputs are finite; a program needn't handle non-finite values.
Results may differ from the reference program's by a relative error of at most 0.0034.
Values may be sent and summed in bfloat16 or wider, within the bound.
A program may use at most 384 MiB of HBM per device.

```python
import math
import jax
import jax.numpy as jnp
from jax import lax

HEADS = 40
CONV = 4
GROUP = 256
INNER = 2560
CONV_DIM = 2816
TOKENS = 16384


def draw_decay_rate(key, part):
    lowest = math.log(0.003 / TOKENS)
    highest = math.log(0.05)
    spread = jax.random.uniform(jax.random.fold_in(key, 14), (HEADS,), jnp.float32, lowest, highest)
    return jnp.exp(spread).astype(jnp.float32)


def level_of(own_key, dims, cuts, smallest, largest):
    def one(dim, shards_of):
        draws = jax.random.uniform(jax.random.fold_in(jax.random.fold_in(own_key, 6), dim), (shards_of,), jnp.float32, smallest / len(cuts), largest / len(cuts))
        return jnp.repeat(jnp.exp(draws), dims[dim] // shards_of).reshape((-1,) + (1,) * (len(dims) - dim - 1))

    gain = one(*cuts[0])
    for cut in cuts[1:]:
        gain = gain * one(*cut)
    return gain


def bell_draw(key, dims, deviation, reach, cuts=(), held_as=jnp.bfloat16):
    gain = level_of(key, dims, cuts, -0.22, 0.18) if cuts else 1.0
    values = jax.random.normal(key, dims, jnp.float32) * deviation * gain
    return jnp.minimum(jnp.maximum(values, -reach), reach).astype(held_as)


def setup_inputs(seed: int = 0, part: int = 0) -> dict:
    arg_keys = jax.random.split(jax.random.key(seed), 8)
    part_splits = jax.random.split(jax.random.fold_in(arg_keys[7], part), 8)
    conv_input = bell_draw(part_splits[0], (TOKENS, CONV_DIM), 1.0, 6.0, ((0, 16),))
    step_raw = bell_draw(part_splits[1], (TOKENS, HEADS), 1.0, 4.0, ((0, 16),))
    conv_weight = bell_draw(arg_keys[2], (CONV, CONV_DIM), 0.5, 3.0, (), jnp.float32)
    conv_bias = bell_draw(arg_keys[3], (CONV_DIM,), 0.5, 3.0, (), jnp.float32)
    step_bias = jnp.clip(jax.random.uniform(arg_keys[4], (HEADS,), jnp.float32, -1.0, 1.0), -1.0, 1.0)
    decay_rate = draw_decay_rate(jax.random.fold_in(arg_keys[7], 71), part)
    norm_gain = jnp.clip(1.0 + 0.18 * jax.random.normal(arg_keys[6], (INNER,), jnp.float32), 0.1, 1.9)
    return {"conv_input": conv_input, "step_raw": step_raw, "conv_weight": conv_weight, "conv_bias": conv_bias, "step_bias": step_bias, "decay_rate": decay_rate, "norm_gain": norm_gain}


def conv_mix(padded, conv_weight, conv_bias, row_count):
    total = jnp.zeros((row_count, padded.shape[1]), jnp.float32) + conv_bias
    for offset in range(conv_weight.shape[0]):
        total = total + padded[offset:offset + row_count].astype(jnp.float32) * conv_weight[offset]
    return jax.nn.silu(total).astype(jnp.bfloat16)

def block_parts(values, inputs_b, inputs_c, step_sizes, log_decay):
    cumulative = jnp.cumsum(log_decay, axis=0)
    scores = jnp.dot(inputs_c, inputs_b.T, preferred_element_type=jnp.float32)
    span_rows = log_decay.shape[0]
    causal = jnp.tril(jnp.ones((span_rows, span_rows), dtype=bool))
    gap_table = cumulative.T[:, :, None] - cumulative.T[:, None, :]
    decay = jnp.where(causal[None], jnp.exp(jnp.where(causal[None], gap_table, 0.0)), 0.0)
    mixing = (scores[None] * decay * step_sizes.T[:, None, :]).astype(jnp.bfloat16)
    mixing = lax.optimization_barrier(mixing)
    within = jnp.einsum('hts,shp->thp', mixing.astype(jnp.float32), values.astype(jnp.float32))
    weights = jnp.exp(cumulative[-1][None, :] - cumulative) * step_sizes
    scaled = (weights[:, :, None] * values.astype(jnp.float32)).astype(jnp.bfloat16)
    scaled = lax.optimization_barrier(scaled)
    update = jnp.einsum('shp,sn->hpn', scaled.astype(jnp.float32), inputs_b.astype(jnp.float32))
    return (cumulative, within, update)

def finish(result, norm_gain):
    flat = result.reshape(result.shape[0], -1)
    scale = lax.rsqrt(lax.optimization_barrier(jnp.mean(flat * flat, axis=-1, keepdims=True)) + 1e-05)
    return (flat * scale * norm_gain).astype(jnp.bfloat16)

def reference(conv_input, step_raw, conv_weight, conv_bias, step_bias, decay_rate, norm_gain):
    total_rows, conv_dim = conv_input.shape
    head_count = decay_rate.shape[0]
    inner = norm_gain.shape[0]
    state_dim = (conv_dim - inner) // 2
    head_size = inner // head_count
    margin = conv_weight.shape[0] - 1
    padded = jnp.concatenate([jnp.zeros((margin, conv_dim), jnp.bfloat16), conv_input], axis=0)
    mixed = conv_mix(padded, conv_weight, conv_bias, total_rows)
    step_sizes = jax.nn.softplus(step_raw.astype(jnp.float32) + step_bias)
    log_decay = -decay_rate * step_sizes
    blocks = total_rows // GROUP
    values = mixed[:, :inner].reshape(blocks, GROUP, head_count, head_size)
    inputs_b = mixed[:, inner:inner + state_dim].reshape(blocks, GROUP, state_dim)
    inputs_c = mixed[:, inner + state_dim:].reshape(blocks, GROUP, state_dim)

    def advance(carried, pieces):
        block_values, block_b, block_c, block_steps, block_logs = pieces
        cumulative, within, update = block_parts(block_values, block_b, block_c, block_steps, block_logs)
        across = jnp.einsum('hpn,tn->thp', carried, block_c.astype(jnp.float32), precision=lax.Precision.HIGHEST)
        across = across * jnp.exp(cumulative)[:, :, None]
        result = finish(within + across, norm_gain)
        carried = jnp.exp(cumulative[-1])[:, None, None] * carried + update
        return (carried, result)
    start_state = jnp.zeros((head_count, head_size, state_dim), jnp.float32)
    final_state, outputs = lax.scan(advance, start_state, (values, inputs_b, inputs_c, step_sizes.reshape(blocks, GROUP, head_count), log_decay.reshape(blocks, GROUP, head_count)))
    return outputs.reshape(total_rows, inner)
```

```python
import functools

import jax
import jax.numpy as jnp
from jax import lax
from jax.experimental import pallas as pl
from jax.experimental.pallas import tpu as pltpu
from jax.sharding import PartitionSpec as P

GROUP = 256
WIDE = 256
LANES = 128
HALO = 8
EDGE = 16
F32, BF16 = jnp.float32, jnp.bfloat16


def dot(left, right):
    return jnp.dot(left, right, preferred_element_type=F32)


def split(value):
    high = value.astype(BF16).astype(F32)
    return high, value - high


def lower_triangle():
    rows = lax.broadcasted_iota(jnp.int32, (GROUP, GROUP), 0)
    columns = lax.broadcasted_iota(jnp.int32, (GROUP, GROUP), 1)
    return rows >= columns


def fill_spread(spread, heads):
    width = spread.shape[1] // heads
    rows = lax.broadcasted_iota(jnp.int32, spread.shape, 0)
    columns = lax.broadcasted_iota(jnp.int32, spread.shape, 1)
    rows = jnp.where(rows >= LANES // 2, rows - LANES // 2, rows)
    start = rows * width
    spread[...] = jnp.where((columns >= start) & (columns < start + width), 1.0, 0.0).astype(BF16)


def front_kernel(
    inner, heads, blocks, count,
    whole_ref, raw_ref, weight_ref, bias_ref, step_bias_ref, rate_ref,
    y_ref, squares_ref,
    inbuf, xb, rows_out, held, scores, b_turned, c_rows, a_packs, b_packs, g_packs, big_packs, spread, pack, square,
    logs_all, chip_logs, chip_decay, own_decay, chip_state,
    state, up_in, first_out, first_in, second_out, second_in, back_out, back_in,
    in_sems, send_sems, halo_recv, log_recv, up_recvs, first_recvs, second_recvs, back_recvs,
):
    place = lax.axis_index("seq")
    chips = count // 2
    owners = chips // 2
    chip, core = place // 2, lax.rem(place, 2)
    lowest = chips // 4
    part = LANES // owners
    half = LANES // 2
    tokens = blocks * GROUP
    tiles = inner // WIDE
    partner = place + 1 - 2 * core

    def peer(step):
        return lax.rem(place + step, count)

    def columns_of(tile):
        if isinstance(tile, int):
            return pl.ds(tile * WIDE, WIDE)
        return pl.ds(pl.multiple_of(tile * WIDE, WIDE), WIDE)

    def send(source, target, send_sem, recv_sem, device):
        return pltpu.make_async_remote_copy(
            src_ref=source, dst_ref=target, send_sem=send_sem, recv_sem=recv_sem,
            device_id={"seq": device}, device_id_type=pl.DeviceIdType.MESH,
        )

    def in_copy(start, width, sem):
        columns = pl.ds(start, width)
        return pltpu.make_async_copy(whole_ref.at[:, columns], inbuf.at[pl.ds(EDGE, tokens), columns], in_sems.at[sem])

    bc_in, x_in = in_copy(inner, WIDE, 0), in_copy(0, inner, 1)

    def y_copy(tile):
        columns = columns_of(tile)
        return pltpu.make_async_copy(rows_out.at[:, columns], y_ref.at[:, columns], in_sems.at[2])

    halo_copy = send(
        whole_ref.at[pl.ds(tokens - EDGE, EDGE)], inbuf.at[pl.ds(0, EDGE)], send_sems.at[0], halo_recv.at[0], peer(1)
    )

    def log_copy(hop):
        return send(logs_all.at[place], logs_all.at[place], send_sems.at[1], log_recv.at[0], peer(hop))

    everyone = logs_all.at[pl.ds(0, count - 1)]
    all_logs = send(everyone, everyone, send_sems.at[1], log_recv.at[0], partner)

    def turned(high, low):
        square[0:heads] = jnp.broadcast_to(high, (heads, LANES))
        square[half : half + heads] = jnp.broadcast_to(low, (heads, LANES))
        return square[...].T[0:8]

    def column(ref):
        square[0:1, 0:heads] = ref[...].reshape(1, heads)
        return jnp.broadcast_to(square[0:1], (LANES, LANES)).T[0:heads, 0:1]

    barrier = pltpu.get_barrier_semaphore()
    for hop in range(1, count):
        pl.semaphore_signal(barrier, inc=1, device_id={"seq": peer(hop)}, device_id_type=pl.DeviceIdType.MESH)
    bc_in.start()
    x_in.start()
    squares_ref[...] = jnp.zeros_like(squares_ref)
    square[...] = jnp.zeros_like(square)
    pack[...] = jnp.zeros_like(pack)
    step_bias, rate = column(step_bias_ref), column(rate_ref)
    square[...] = jnp.zeros_like(square)
    shifted = raw_ref[...].astype(F32) + step_bias
    step = jnp.maximum(shifted, 0.0) + jnp.log(1.0 + jnp.exp(-jnp.abs(shifted)))
    logs = -rate * step
    total = jnp.sum(logs, axis=1, keepdims=True)
    logs_all[place] = turned(total, jnp.zeros_like(total))
    pl.semaphore_wait(barrier, count - 1)

    @pl.when(place < count - 1)
    def _():
        halo_copy.start()

    for hop in range(1, count):
        log_copy(hop).start()
    fill_spread(spread, heads)
    ones = lower_triangle().astype(F32).T.astype(BF16)
    high, rest = split(logs)
    middle, low = split(rest)
    before = jnp.zeros((heads, 1), F32)
    for block in range(blocks):
        span = slice(block * GROUP, (block + 1) * GROUP)
        cum = dot(high[:, span].astype(BF16), ones) + (
            dot(middle[:, span].astype(BF16), ones) + dot(low[:, span].astype(BF16), ones)
        )
        end = cum[:, GROUP - 1 : GROUP]
        mid = 0.5 * end
        first, second = split(jnp.exp(cum - mid))
        pack[0:heads, :] = first
        pack[half : half + heads, :] = second
        a_packs[span] = pack[...].T.astype(BF16)
        first, second = split(jnp.exp(mid - cum) * step[:, span])
        pack[0:heads, :] = first
        pack[half : half + heads, :] = second
        b_packs[span] = pack[...].T.astype(BF16)
        first, second = split(jnp.exp(mid))
        g_packs[8 * block : 8 * block + 8] = turned(first, second)
        first, second = split(jnp.exp(before + mid))
        big_packs[8 * block : 8 * block + 8] = turned(first, second)
        before = before + end

    def mix(block, tile):
        pieces = []
        top = block * GROUP
        for piece in range(WIDE // LANES):
            if isinstance(tile, int):
                lanes = pl.ds(tile * WIDE + piece * LANES, LANES)
            else:
                lanes = pl.ds(pl.multiple_of(tile * WIDE + piece * LANES, LANES), LANES)
            rows = jnp.concatenate(
                [inbuf[top : top + EDGE, lanes].astype(F32)[EDGE - HALO :], inbuf[top + EDGE : top + EDGE + GROUP, lanes].astype(F32)],
                axis=0,
            )
            weights = 0.5 * weight_ref[:, lanes]
            total = rows * weights[0:1]
            for k in range(1, 4):
                total = pltpu.roll(total, 1, 0) + rows * weights[k : k + 1]
            value = total[HALO:] + 0.5 * bias_ref[lanes].reshape(1, LANES)
            pieces.append(value + value * jnp.tanh(value))
        return jnp.concatenate(pieces, axis=1)

    bc_in.wait()

    triangle = lower_triangle()

    def side_block(block):
        span = slice(block * GROUP, (block + 1) * GROUP)
        bc = mix(block, tiles).astype(BF16)
        b, c = bc[:, :LANES], bc[:, LANES:]
        c_rows[span] = c
        turn = b.astype(F32).T.astype(BF16)
        b_turned[block] = turn
        scores[block] = jnp.where(triangle, dot(c, turn), 0.0).astype(BF16)

    for block in range(1, blocks):
        side_block(block)
    x_in.wait()

    @pl.when(place > 0)
    def _():
        halo_copy.wait_recv()

    @pl.when(place == 0)
    def _():
        inbuf[0:EDGE] = jnp.zeros((EDGE, inbuf.shape[1]), BF16)

    @pl.when(chip == 0)
    def _():
        second_in[...] = jnp.zeros_like(second_in)

    side_block(0)

    def front_tile(tile):
        columns = columns_of(tile)
        wide = spread[:, columns]
        g_all = dot(g_packs[...].astype(BF16), wide)
        carried = None
        for block in range(blocks):
            span = slice(block * GROUP, (block + 1) * GROUP)
            scaled = (mix(block, tile) * dot(b_packs[span], wide)).astype(BF16)
            xb[span, columns] = scaled
            update = dot(b_turned[block], scaled)
            g = g_all[8 * block : 8 * block + 1]
            if block == 0:
                carried = g * update
            else:
                kept = g * carried
                held[block - 1, :, columns] = kept.astype(BF16)
                carried = g * (kept + update)
        state[tile] = carried

    def back_tile(tile):
        columns = columns_of(tile)
        wide = spread[:, columns]
        big_all = dot(big_packs[...].astype(BF16), wide)
        arrived = back_in[tile]
        for block in range(blocks):
            span = slice(block * GROUP, (block + 1) * GROUP)
            start = big_all[8 * block : 8 * block + 1] * arrived
            if block > 0:
                start = start + held[block - 1, :, columns].astype(F32)
            value = dot(scores[block], xb[span, columns]) + dot(c_rows[span], start.astype(BF16))
            y = value * dot(a_packs[span], wide)
            rows_out[span, columns] = y.astype(BF16)
            own = y * y
            own = own[:, :LANES] + own[:, LANES:]
            squares_ref[span] = squares_ref[span] + own
        y_copy(tile).start()

    def leads(tile):
        return lax.rem(tile + tiles, 2) == core

    def up_copy(tile):
        return send(state.at[tile], up_in.at[tile], send_sems.at[2], up_recvs.at[tile // 2], partner)

    def back_copy(tile):
        return send(back_out.at[tile], back_in.at[tile], send_sems.at[3], back_recvs.at[tile // 2], partner)

    def first_copy(tile, owner):
        return send(
            first_out.at[tile, owner], first_in.at[tile, chip],
            send_sems.at[4], first_recvs.at[tile // 2], 2 * (lowest + owner) + core,
        )

    def first_arrivals(tile):
        slots = first_in.at[tile, pl.ds(0, chips - 2)]
        return send(slots, slots, send_sems.at[4], first_recvs.at[tile // 2], partner)

    def second_copy(tile, other):
        return send(
            second_out.at[tile, other], second_in.at[tile, chip - lowest],
            send_sems.at[5], second_recvs.at[tile // 2], 2 * other + core,
        )

    def second_arrivals(tile, number):
        slots = second_in.at[tile, pl.ds(0, number)]
        return send(slots, slots, send_sems.at[5], second_recvs.at[tile // 2], partner)

    def rows_of(owner):
        return slice(owner * part, (owner + 1) * part)

    owning = (chip >= lowest) & (chip < lowest + owners)

    def logs_finish():
        all_logs.wait_recv()
        lane = lax.broadcasted_iota(jnp.int32, (8, LANES), 1)

        def packed(log):
            first, second = split(jnp.exp(log))
            return jnp.where(lane < half, first, pltpu.roll(second, half, 1))

        for other in range(chips):
            chip_logs[other : other + 1] = (logs_all[2 * other] + logs_all[2 * other + 1])[0:1]
        chip_pack = jnp.concatenate([packed(chip_logs[row : row + 8]) for row in range(0, chips, 8)], axis=0).astype(BF16)
        own_pack = jnp.concatenate([packed(logs_all[2 * chip]), packed(logs_all[2 * chip + 1])], axis=0).astype(BF16)
        for tile in range(tiles):
            columns = columns_of(tile)
            chip_decay[:, columns] = dot(chip_pack, spread[:, columns])
            own_decay[:, columns] = dot(own_pack, spread[:, columns])

    def pair_start(tile):
        @pl.when(jnp.logical_not(leads(tile)))
        def _():
            up_copy(tile).start()

    def first_step(tile):
        @pl.when(leads(tile))
        def _():
            up_copy(tile).wait_recv()
            got, mine = up_in[tile], state[tile]
            earlier = jnp.where(core == 0, mine, got)
            later = jnp.where(core == 0, got, mine)
            state[tile] = earlier
            chip_state[...] = own_decay[8:16, columns_of(tile)][0:1] * earlier + later
            for owner in range(owners):
                first_out[tile, owner] = chip_state[rows_of(owner)].astype(BF16)

                @pl.when((chip != lowest + owner) & (chip < chips - 1))
                def _():
                    first_copy(tile, owner).start()

                @pl.when(chip == lowest + owner)
                def _():
                    first_in[tile, chip] = first_out[tile, owner]

    def second_step(tile):
        @pl.when(leads(tile) & owning)
        def _():
            first_arrivals(tile).wait_recv()
            prefix = jnp.zeros((part, WIDE), F32)
            decays = chip_decay[:, columns_of(tile)]
            for other in range(chips):
                if other > 0:
                    second_out[tile, other] = prefix.astype(BF16)

                    @pl.when(chip != other)
                    def _():
                        second_copy(tile, other).start()

                    @pl.when(chip == other)
                    def _():
                        second_in[tile, chip - lowest] = second_out[tile, other]

                if other < chips - 1:
                    prefix = decays[other : other + 1] * prefix + first_in[tile, other].astype(F32)

    def third_step(tile):
        @pl.when(leads(tile))
        def _():
            @pl.when(owning)
            def _():
                second_arrivals(tile, owners - 1).wait_recv()

            @pl.when((chip > 0) & jnp.logical_not(owning))
            def _():
                second_arrivals(tile, owners).wait_recv()

            for owner in range(owners):
                chip_state[rows_of(owner)] = second_in[tile, owner].astype(F32)
            earlier = chip_state[...]
            later = own_decay[0:8, columns_of(tile)][0:1] * earlier + state[tile]
            back_out[tile] = jnp.where(core == 0, later, earlier)
            back_copy(tile).start()
            back_in[tile] = jnp.where(core == 0, earlier, later)

    def fourth_step(tile):
        @pl.when(jnp.logical_not(leads(tile)))
        def _():
            back_copy(tile).wait_recv()

    last = tiles - 1

    def front_body(tick, _):
        front_tile(tick)
        pair_start(tick)

        @pl.when(tick == 1)
        def _():
            logs_finish()

        @pl.when(tick >= 1)
        def _():
            first_step(tick - 1)

        @pl.when(tick >= 4)
        def _():
            second_step(tick - 4)

        @pl.when(tick >= 8)
        def _():
            third_step(tick - 8)

        return 0

    lax.fori_loop(0, tiles, front_body, 0)

    def back_body(tile, _):
        @pl.when(tile == 1)
        def _():
            first_step(last)

        @pl.when(tile + tiles - 4 < last)
        def _():
            second_step(tile + tiles - 4)

        @pl.when(tile == tiles // 2)
        def _():
            second_step(last)

        @pl.when(tile + tiles - 8 < last)
        def _():
            third_step(tile + tiles - 8)

        @pl.when(tile == last)
        def _():
            third_step(last)

        fourth_step(tile)
        back_tile(tile)
        return 0

    lax.fori_loop(0, tiles, back_body, 0)

    @pl.when(place < count - 1)
    def _():
        halo_copy.wait_send()

    all_logs.wait_send()
    led = tiles // 2

    def sent(ref, sem):
        send(ref, ref, sem, up_recvs.at[0], partner).wait_send()

    sent(state.at[pl.ds(0, led)], send_sems.at[2])
    sent(back_out.at[pl.ds(0, led)], send_sems.at[3])

    @pl.when(owning)
    def _():
        sent(first_out.at[pl.ds(0, led), pl.ds(0, owners - 1)], send_sems.at[4])
        sent(second_out.at[pl.ds(0, led), pl.ds(0, chips - 2)], send_sems.at[5])

    @pl.when(jnp.logical_not(owning) & (chip < chips - 1))
    def _():
        sent(first_out.at[pl.ds(0, led)], send_sems.at[4])

    pltpu.make_async_copy(rows_out, y_ref, in_sems.at[2]).wait()


def back_kernel(inner, y_ref, squares_ref, gain_ref, out_ref):
    mean = jnp.sum(squares_ref[...], axis=1, keepdims=True) * (1.0 / inner)
    scale = lax.rsqrt(mean + 1e-05)
    for start in range(0, inner, LANES):
        columns = slice(start, start + LANES)
        out_ref[:, columns] = (y_ref[:, columns].astype(F32) * scale * gain_ref[columns].reshape(1, LANES)).astype(BF16)


def per_device(conv_input, step_raw, conv_weight, conv_bias, step_bias, decay_rate, norm_gain):
    tokens, conv_dim = conv_input.shape
    heads, inner = decay_rate.shape[0], norm_gain.shape[0]
    blocks, tiles = tokens // GROUP, inner // WIDE
    count = lax.axis_size("seq")
    chips = count // 2
    owners = chips // 2
    part = LANES // owners

    def vmem(*shape, dtype=BF16):
        return pltpu.VMEM(shape, dtype)

    shape = jax.ShapeDtypeStruct
    inside, anywhere = pl.BlockSpec(memory_space=pltpu.VMEM), pl.BlockSpec(memory_space=pl.ANY)
    dma = pltpu.SemaphoreType.DMA
    y, squares = pl.pallas_call(
        functools.partial(front_kernel, inner, heads, blocks, count),
        in_specs=[anywhere] + [inside] * 5,
        out_specs=[anywhere, inside],
        out_shape=[shape((tokens, inner), BF16), shape((tokens, LANES), F32)],
        scratch_shapes=[
            vmem(EDGE + tokens, conv_dim), vmem(tokens, inner), vmem(tokens, inner), vmem(blocks - 1, LANES, inner),
            vmem(blocks, GROUP, GROUP), vmem(blocks, LANES, GROUP), vmem(tokens, LANES), vmem(tokens, LANES),
            vmem(tokens, LANES), vmem(8 * blocks, LANES, dtype=F32), vmem(8 * blocks, LANES, dtype=F32),
            vmem(LANES, inner), vmem(LANES, GROUP, dtype=F32), vmem(LANES, LANES, dtype=F32),
            vmem(count, 8, LANES, dtype=F32), vmem(chips, LANES, dtype=F32), vmem(chips, inner, dtype=F32),
            vmem(16, inner, dtype=F32), vmem(LANES, WIDE, dtype=F32),
            vmem(tiles, LANES, WIDE, dtype=F32), vmem(tiles, LANES, WIDE, dtype=F32),
            vmem(tiles, owners, part, WIDE), vmem(tiles, chips, part, WIDE),
            vmem(tiles, chips, part, WIDE), vmem(tiles, owners, part, WIDE),
            vmem(tiles, LANES, WIDE, dtype=F32), vmem(tiles, LANES, WIDE, dtype=F32),
            dma((3,)), dma((6,)), dma((1,)), dma((1,)), dma((tiles // 2,)), dma((tiles // 2,)), dma((tiles // 2,)), dma((tiles // 2,)),
        ],
        compiler_params=pltpu.CompilerParams(collective_id=0, has_side_effects=True, vmem_limit_bytes=60 * 1024 * 1024),
        name="front",
    )(conv_input, step_raw.T, conv_weight, conv_bias, step_bias, decay_rate)
    rows = 2 * GROUP
    return pl.pallas_call(
        functools.partial(back_kernel, inner),
        grid=(tokens // rows,),
        in_specs=[
            pl.BlockSpec((rows, inner), lambda i: (i, 0)), pl.BlockSpec((rows, LANES), lambda i: (i, 0)),
            pl.BlockSpec((inner,), lambda i: (0,)),
        ],
        out_specs=pl.BlockSpec((rows, inner), lambda i: (i, 0)),
        out_shape=shape((tokens, inner), BF16),
        name="back",
    )(y, squares, norm_gain)


def solution(mesh):
    placed = (P(("parts", "seq"), None), P(("parts", "seq"), None), P(), P(), P(), P(), P())
    return jax.shard_map(
        per_device, mesh=mesh, in_specs=placed, out_specs=P(("parts", "seq"), None), check_vma=False
    )
```

```python
import functools

import jax
import jax.numpy as jnp
from jax import lax
from jax.experimental import pallas as pl
from jax.experimental.pallas import tpu as pltpu
from jax.sharding import PartitionSpec as P

GROUP = 256
WIDE = 256
LANES = 128
HALO = 8
EDGE = 16
EARLY = 3
F32, BF16 = jnp.float32, jnp.bfloat16


def dot(left, right):
    return jnp.dot(left, right, preferred_element_type=F32)


def split(value):
    high = value.astype(BF16).astype(F32)
    return high, value - high


def lower_triangle():
    rows = lax.broadcasted_iota(jnp.int32, (GROUP, GROUP), 0)
    columns = lax.broadcasted_iota(jnp.int32, (GROUP, GROUP), 1)
    return rows >= columns


def fill_spread(spread, heads):
    width = spread.shape[1] // heads
    rows = lax.broadcasted_iota(jnp.int32, spread.shape, 0)
    columns = lax.broadcasted_iota(jnp.int32, spread.shape, 1)
    rows = jnp.where(rows >= LANES // 2, rows - LANES // 2, rows)
    start = rows * width
    spread[...] = jnp.where((columns >= start) & (columns < start + width), 1.0, 0.0).astype(BF16)


def front_kernel(
    inner, heads, blocks, count,
    whole_ref, raw_ref, weight_ref, bias_ref, step_bias_ref, rate_ref,
    y_ref, squares_ref,
    inbuf, taps, local, updates, rows_out, held, mixer, c_rows, a_packs, b_packs, g_packs, big_packs, spread, pack, square,
    logs_all, chip_logs, chip_decay, own_decay, chip_state,
    state, up_in, first_out, first_in, second_out, second_in, back_out, back_in,
    in_sems, send_sems, halo_recv, log_recv, up_recvs, first_recvs, second_recvs, back_recvs,
):
    place = lax.axis_index("seq")
    chips = count // 2
    owners = chips // 2
    chip, core = place // 2, lax.rem(place, 2)
    lowest = chips // 4
    part = LANES // owners
    half = LANES // 2
    tokens = blocks * GROUP
    tiles = inner // WIDE
    early = updates.shape[0]
    partner = place + 1 - 2 * core

    def peer(step):
        return lax.rem(place + step, count)

    def columns_of(tile):
        if isinstance(tile, int):
            return pl.ds(tile * WIDE, WIDE)
        return pl.ds(pl.multiple_of(tile * WIDE, WIDE), WIDE)

    def send(source, target, send_sem, recv_sem, device):
        return pltpu.make_async_remote_copy(
            src_ref=source, dst_ref=target, send_sem=send_sem, recv_sem=recv_sem,
            device_id={"seq": device}, device_id_type=pl.DeviceIdType.MESH,
        )

    def in_copy(start, width, sem):
        columns = pl.ds(start, width)
        return pltpu.make_async_copy(whole_ref.at[:, columns], inbuf.at[pl.ds(EDGE, tokens), columns], in_sems.at[sem])

    bc_in, x_in = in_copy(inner, WIDE, 0), in_copy(0, inner, 1)

    def y_copy(tile):
        columns = columns_of(tile)
        return pltpu.make_async_copy(rows_out.at[:, columns], y_ref.at[:, columns], in_sems.at[2])

    halo_copy = send(
        whole_ref.at[pl.ds(tokens - EDGE, EDGE)], inbuf.at[pl.ds(0, EDGE)], send_sems.at[0], halo_recv.at[0], peer(1)
    )

    def log_copy(hop):
        return send(logs_all.at[place], logs_all.at[place], send_sems.at[1], log_recv.at[0], peer(hop))

    everyone = logs_all.at[pl.ds(0, count - 1)]
    all_logs = send(everyone, everyone, send_sems.at[1], log_recv.at[0], partner)

    def turned(high, low):
        square[0:heads] = jnp.broadcast_to(high, (heads, LANES))
        square[half : half + heads] = jnp.broadcast_to(low, (heads, LANES))
        return square[...].T[0:8]

    def column(ref):
        square[0:1, 0:heads] = ref[...].reshape(1, heads)
        return jnp.broadcast_to(square[0:1], (LANES, LANES)).T[0:heads, 0:1]

    barrier = pltpu.get_barrier_semaphore()
    for hop in range(1, count):
        pl.semaphore_signal(barrier, inc=1, device_id={"seq": peer(hop)}, device_id_type=pl.DeviceIdType.MESH)
    bc_in.start()
    x_in.start()
    squares_ref[...] = jnp.zeros_like(squares_ref)
    square[...] = jnp.zeros_like(square)
    pack[...] = jnp.zeros_like(pack)
    step_bias, rate = column(step_bias_ref), column(rate_ref)
    square[...] = jnp.zeros_like(square)
    shifted = raw_ref[...].astype(F32) + step_bias
    step = jnp.maximum(shifted, 0.0) + jnp.log(1.0 + jnp.exp(-jnp.abs(shifted)))
    logs = -rate * step
    total = jnp.sum(logs, axis=1, keepdims=True)
    logs_all[place] = turned(total, jnp.zeros_like(total))
    pl.semaphore_wait(barrier, count - 1)

    @pl.when(place < count - 1)
    def _():
        halo_copy.start()

    for hop in range(1, count):
        log_copy(hop).start()
    fill_spread(spread, heads)
    ones = lower_triangle().astype(F32).T.astype(BF16)
    high, rest = split(logs)
    middle, low = split(rest)
    before = jnp.zeros((heads, 1), F32)
    for block in range(blocks):
        span = slice(block * GROUP, (block + 1) * GROUP)
        cum = dot(high[:, span].astype(BF16), ones) + (
            dot(middle[:, span].astype(BF16), ones) + dot(low[:, span].astype(BF16), ones)
        )
        end = cum[:, GROUP - 1 : GROUP]
        mid = 0.5 * end
        first, second = split(jnp.exp(cum - mid))
        pack[0:heads, :] = first
        pack[half : half + heads, :] = second
        a_packs[span] = pack[...].T.astype(BF16)
        first, second = split(jnp.exp(mid - cum) * step[:, span])
        pack[0:heads, :] = first
        pack[half : half + heads, :] = second
        b_packs[span] = pack[...].T.astype(BF16)
        first, second = split(jnp.exp(mid))
        g_packs[8 * block : 8 * block + 8] = turned(first, second)
        first, second = split(jnp.exp(before + mid))
        big_packs[8 * block : 8 * block + 8] = turned(first, second)
        before = before + end

    def mix(block, tile):
        pieces = []
        top = block * GROUP
        for piece in range(WIDE // LANES):
            if isinstance(tile, int):
                lanes = pl.ds(tile * WIDE + piece * LANES, LANES)
            else:
                lanes = pl.ds(pl.multiple_of(tile * WIDE + piece * LANES, LANES), LANES)
            slot = block * (WIDE // LANES) + piece
            rows = inbuf[top + EDGE : top + EDGE + GROUP, lanes].astype(F32)
            taps[slot, 0:HALO] = inbuf[top : top + EDGE, lanes].astype(F32)[EDGE - HALO :]
            taps[slot, HALO:] = rows
            weights = 0.5 * weight_ref[:, lanes]
            value = rows * weights[3:4] + 0.5 * bias_ref[lanes].reshape(1, LANES)
            for k in range(3):
                value = value + taps[slot, HALO - 3 + k : HALO - 3 + k + GROUP] * weights[k : k + 1]
            pieces.append(value + value * jnp.tanh(value))
        return jnp.concatenate(pieces, axis=1)

    bc_in.wait()

    triangle = lower_triangle()

    def side_block(block):
        span = slice(block * GROUP, (block + 1) * GROUP)
        bc = mix(block, tiles).astype(BF16)
        b, c = bc[:, :LANES], bc[:, LANES:]
        c_rows[span] = c
        turn = b.astype(F32).T.astype(BF16)
        mixer[block, 0:GROUP] = jnp.where(triangle, dot(c, turn), 0.0).astype(BF16)
        mixer[block, GROUP:] = turn

    def front_block(tile, block):
        columns = columns_of(tile)
        span = slice(block * GROUP, (block + 1) * GROUP)
        scaled = (mix(block, tile) * dot(b_packs[span], spread[:, columns])).astype(BF16)
        product = dot(mixer[block], scaled)
        local[span, columns] = product[:GROUP]
        return product[GROUP:]

    def early_body(tile, _):
        for block in range(1, blocks):
            updates[tile, block - 1] = front_block(tile, block)
        return 0

    for block in range(1, blocks):
        side_block(block)
    x_in.wait()
    lax.fori_loop(0, early, early_body, 0)

    @pl.when(place > 0)
    def _():
        halo_copy.wait_recv()

    @pl.when(place == 0)
    def _():
        inbuf[0:EDGE] = jnp.zeros((EDGE, inbuf.shape[1]), BF16)

    @pl.when(chip == 0)
    def _():
        second_in[...] = jnp.zeros_like(second_in)

    side_block(0)

    def front_tile(tile, ready):
        columns = columns_of(tile)
        wide = spread[:, columns]
        g_all = dot(g_packs[...].astype(BF16), wide)
        carried = None
        for block in range(blocks):
            update = updates[tile, block - 1] if ready and block > 0 else front_block(tile, block)
            g = g_all[8 * block : 8 * block + 1]
            if block == 0:
                carried = g * update
            else:
                kept = g * carried
                held[block - 1, :, columns] = kept.astype(BF16)
                carried = g * (kept + update)
        state[tile] = carried

    def back_tile(tile):
        columns = columns_of(tile)
        wide = spread[:, columns]
        big_all = dot(big_packs[...].astype(BF16), wide)
        arrived = back_in[tile]
        for block in range(blocks):
            span = slice(block * GROUP, (block + 1) * GROUP)
            start = big_all[8 * block : 8 * block + 1] * arrived
            if block > 0:
                start = start + held[block - 1, :, columns].astype(F32)
            value = local[span, columns] + dot(c_rows[span], start.astype(BF16))
            y = value * dot(a_packs[span], wide)
            rows_out[span, columns] = y.astype(BF16)
            own = y * y
            own = own[:, :LANES] + own[:, LANES:]
            squares_ref[span] = squares_ref[span] + own
        y_copy(tile).start()

    def leads(tile):
        return lax.rem(tile + tiles, 2) == core

    def up_copy(tile):
        return send(state.at[tile], up_in.at[tile], send_sems.at[2], up_recvs.at[tile // 2], partner)

    def back_copy(tile):
        return send(back_out.at[tile], back_in.at[tile], send_sems.at[3], back_recvs.at[tile // 2], partner)

    def first_copy(tile, owner):
        return send(
            first_out.at[tile, owner], first_in.at[tile, chip],
            send_sems.at[4], first_recvs.at[tile // 2], 2 * (lowest + owner) + core,
        )

    def first_arrivals(tile):
        slots = first_in.at[tile, pl.ds(0, chips - 2)]
        return send(slots, slots, send_sems.at[4], first_recvs.at[tile // 2], partner)

    def second_copy(tile, other):
        return send(
            second_out.at[tile, other], second_in.at[tile, chip - lowest],
            send_sems.at[5], second_recvs.at[tile // 2], 2 * other + core,
        )

    def second_arrivals(tile, number):
        slots = second_in.at[tile, pl.ds(0, number)]
        return send(slots, slots, send_sems.at[5], second_recvs.at[tile // 2], partner)

    def rows_of(owner):
        return slice(owner * part, (owner + 1) * part)

    owning = (chip >= lowest) & (chip < lowest + owners)

    def logs_finish():
        all_logs.wait_recv()
        lane = lax.broadcasted_iota(jnp.int32, (8, LANES), 1)

        def packed(log):
            first, second = split(jnp.exp(log))
            return jnp.where(lane < half, first, pltpu.roll(second, half, 1))

        for other in range(chips):
            chip_logs[other : other + 1] = (logs_all[2 * other] + logs_all[2 * other + 1])[0:1]
        chip_pack = jnp.concatenate([packed(chip_logs[row : row + 8]) for row in range(0, chips, 8)], axis=0).astype(BF16)
        own_pack = jnp.concatenate([packed(logs_all[2 * chip]), packed(logs_all[2 * chip + 1])], axis=0).astype(BF16)
        for tile in range(tiles):
            columns = columns_of(tile)
            chip_decay[:, columns] = dot(chip_pack, spread[:, columns])
            own_decay[:, columns] = dot(own_pack, spread[:, columns])

    def pair_start(tile):
        @pl.when(jnp.logical_not(leads(tile)))
        def _():
            up_copy(tile).start()

    def first_step(tile):
        @pl.when(leads(tile))
        def _():
            up_copy(tile).wait_recv()
            got, mine = up_in[tile], state[tile]
            earlier = jnp.where(core == 0, mine, got)
            later = jnp.where(core == 0, got, mine)
            state[tile] = earlier
            chip_state[...] = own_decay[8:16, columns_of(tile)][0:1] * earlier + later
            for owner in range(owners):
                first_out[tile, owner] = chip_state[rows_of(owner)].astype(BF16)

                @pl.when((chip != lowest + owner) & (chip < chips - 1))
                def _():
                    first_copy(tile, owner).start()

                @pl.when(chip == lowest + owner)
                def _():
                    first_in[tile, chip] = first_out[tile, owner]

    def second_step(tile):
        @pl.when(leads(tile) & owning)
        def _():
            first_arrivals(tile).wait_recv()
            prefix = jnp.zeros((part, WIDE), F32)
            decays = chip_decay[:, columns_of(tile)]
            for other in range(chips):
                if other > 0:
                    second_out[tile, other] = prefix.astype(BF16)

                    @pl.when(chip != other)
                    def _():
                        second_copy(tile, other).start()

                    @pl.when(chip == other)
                    def _():
                        second_in[tile, chip - lowest] = second_out[tile, other]

                if other < chips - 1:
                    prefix = decays[other : other + 1] * prefix + first_in[tile, other].astype(F32)

    def third_step(tile):
        @pl.when(leads(tile))
        def _():
            @pl.when(owning)
            def _():
                second_arrivals(tile, owners - 1).wait_recv()

            @pl.when((chip > 0) & jnp.logical_not(owning))
            def _():
                second_arrivals(tile, owners).wait_recv()

            for owner in range(owners):
                chip_state[rows_of(owner)] = second_in[tile, owner].astype(F32)
            earlier = chip_state[...]
            later = own_decay[0:8, columns_of(tile)][0:1] * earlier + state[tile]
            back_out[tile] = jnp.where(core == 0, later, earlier)
            back_copy(tile).start()
            back_in[tile] = jnp.where(core == 0, earlier, later)

    def fourth_step(tile):
        @pl.when(jnp.logical_not(leads(tile)))
        def _():
            back_copy(tile).wait_recv()

    last = tiles - 1

    def early_front_body(tick, _):
        front_tile(tick, True)
        pair_start(tick)

        @pl.when(tick == 1)
        def _():
            logs_finish()

        @pl.when(tick >= 1)
        def _():
            first_step(tick - 1)

        return 0

    def front_body(tick, _):
        front_tile(tick, False)
        pair_start(tick)
        first_step(tick - 1)

        @pl.when(tick >= 5)
        def _():
            second_step(tick - 5)

        @pl.when(tick >= 9)
        def _():
            third_step(tick - 9)

        return 0

    lax.fori_loop(0, early, early_front_body, 0)
    lax.fori_loop(early, tiles, front_body, 0)

    def back_body(tile, _):
        @pl.when(tile == 1)
        def _():
            first_step(last)

        @pl.when(tile + tiles - 5 < last)
        def _():
            second_step(tile + tiles - 5)

        @pl.when(tile == tiles // 2)
        def _():
            second_step(last)

        @pl.when(tile + tiles - 9 < last)
        def _():
            third_step(tile + tiles - 9)

        @pl.when(tile == last)
        def _():
            third_step(last)

        fourth_step(tile)
        back_tile(tile)
        return 0

    lax.fori_loop(0, tiles, back_body, 0)

    @pl.when(place < count - 1)
    def _():
        halo_copy.wait_send()

    all_logs.wait_send()
    led = tiles // 2

    def sent(ref, sem):
        send(ref, ref, sem, up_recvs.at[0], partner).wait_send()

    sent(state.at[pl.ds(0, led)], send_sems.at[2])
    sent(back_out.at[pl.ds(0, led)], send_sems.at[3])

    @pl.when(owning)
    def _():
        sent(first_out.at[pl.ds(0, led), pl.ds(0, owners - 1)], send_sems.at[4])
        sent(second_out.at[pl.ds(0, led), pl.ds(0, chips - 2)], send_sems.at[5])

    @pl.when(jnp.logical_not(owning) & (chip < chips - 1))
    def _():
        sent(first_out.at[pl.ds(0, led)], send_sems.at[4])

    pltpu.make_async_copy(rows_out, y_ref, in_sems.at[2]).wait()


def back_kernel(inner, y_ref, squares_ref, gain_ref, out_ref):
    mean = jnp.sum(squares_ref[...], axis=1, keepdims=True) * (1.0 / inner)
    scale = lax.rsqrt(mean + 1e-05)
    for start in range(0, inner, LANES):
        columns = slice(start, start + LANES)
        out_ref[:, columns] = (y_ref[:, columns].astype(F32) * scale * gain_ref[columns].reshape(1, LANES)).astype(BF16)


def per_device(conv_input, step_raw, conv_weight, conv_bias, step_bias, decay_rate, norm_gain):
    tokens, conv_dim = conv_input.shape
    heads, inner = decay_rate.shape[0], norm_gain.shape[0]
    blocks, tiles = tokens // GROUP, inner // WIDE
    count = lax.axis_size("seq")
    chips = count // 2
    owners = chips // 2
    part = LANES // owners

    def vmem(*shape, dtype=BF16):
        return pltpu.VMEM(shape, dtype)

    shape = jax.ShapeDtypeStruct
    inside, anywhere = pl.BlockSpec(memory_space=pltpu.VMEM), pl.BlockSpec(memory_space=pl.ANY)
    dma = pltpu.SemaphoreType.DMA
    y, squares = pl.pallas_call(
        functools.partial(front_kernel, inner, heads, blocks, count),
        in_specs=[anywhere] + [inside] * 5,
        out_specs=[anywhere, inside],
        out_shape=[shape((tokens, inner), BF16), shape((tokens, LANES), F32)],
        scratch_shapes=[
            vmem(EDGE + tokens, conv_dim), vmem(blocks * WIDE // LANES, HALO + GROUP, LANES, dtype=F32), vmem(tokens, inner, dtype=F32),
            vmem(EARLY, blocks - 1, LANES, WIDE, dtype=F32), vmem(tokens, inner), vmem(blocks - 1, LANES, inner),
            vmem(blocks, GROUP + LANES, GROUP), vmem(tokens, LANES), vmem(tokens, LANES),
            vmem(tokens, LANES), vmem(8 * blocks, LANES, dtype=F32), vmem(8 * blocks, LANES, dtype=F32),
            vmem(LANES, inner), vmem(LANES, GROUP, dtype=F32), vmem(LANES, LANES, dtype=F32),
            vmem(count, 8, LANES, dtype=F32), vmem(chips, LANES, dtype=F32), vmem(chips, inner, dtype=F32),
            vmem(16, inner, dtype=F32), vmem(LANES, WIDE, dtype=F32),
            vmem(tiles, LANES, WIDE, dtype=F32), vmem(tiles, LANES, WIDE, dtype=F32),
            vmem(tiles, owners, part, WIDE), vmem(tiles, chips, part, WIDE),
            vmem(tiles, chips, part, WIDE), vmem(tiles, owners, part, WIDE),
            vmem(tiles, LANES, WIDE, dtype=F32), vmem(tiles, LANES, WIDE, dtype=F32),
            dma((3,)), dma((6,)), dma((1,)), dma((1,)), dma((tiles // 2,)), dma((tiles // 2,)), dma((tiles // 2,)), dma((tiles // 2,)),
        ],
        compiler_params=pltpu.CompilerParams(collective_id=0, has_side_effects=True, vmem_limit_bytes=60 * 1024 * 1024),
        name="front",
    )(conv_input, step_raw.T, conv_weight, conv_bias, step_bias, decay_rate)
    rows = 2 * GROUP
    return pl.pallas_call(
        functools.partial(back_kernel, inner),
        grid=(tokens // rows,),
        in_specs=[
            pl.BlockSpec((rows, inner), lambda i: (i, 0)), pl.BlockSpec((rows, LANES), lambda i: (i, 0)),
            pl.BlockSpec((inner,), lambda i: (0,)),
        ],
        out_specs=pl.BlockSpec((rows, inner), lambda i: (i, 0)),
        out_shape=shape((tokens, inner), BF16),
        name="back",
    )(y, squares, norm_gain)


def solution(mesh):
    placed = (P(("parts", "seq"), None), P(("parts", "seq"), None), P(), P(), P(), P(), P())
    return jax.shard_map(
        per_device, mesh=mesh, in_specs=placed, out_specs=P(("parts", "seq"), None), check_vma=False
    )
```

```python
import functools

import jax
import jax.numpy as jnp
from jax import lax
from jax.experimental import pallas as pl
from jax.experimental.pallas import tpu as pltpu
from jax.sharding import PartitionSpec as P

GROUP = 256
WIDE = 256
LANES = 128
HALO = 8
EDGE = 16
EARLY = 3
F32, BF16 = jnp.float32, jnp.bfloat16


def dot(left, right):
    return jnp.dot(left, right, preferred_element_type=F32)


def split(value):
    high = value.astype(BF16).astype(F32)
    return high, value - high


def lower_triangle():
    rows = lax.broadcasted_iota(jnp.int32, (GROUP, GROUP), 0)
    columns = lax.broadcasted_iota(jnp.int32, (GROUP, GROUP), 1)
    return rows >= columns


def fill_spread(spread, heads):
    width = spread.shape[1] // heads
    rows = lax.broadcasted_iota(jnp.int32, spread.shape, 0)
    columns = lax.broadcasted_iota(jnp.int32, spread.shape, 1)
    rows = jnp.where(rows >= LANES // 2, rows - LANES // 2, rows)
    start = rows * width
    spread[...] = jnp.where((columns >= start) & (columns < start + width), 1.0, 0.0).astype(BF16)


def front_kernel(
    inner, heads, blocks, count,
    whole_ref, raw_ref, weight_ref, bias_ref, step_bias_ref, rate_ref,
    y_ref, squares_out,
    squares_ref, inbuf, taps, local, updates, rows_out, held, mixer, c_rows, a_packs, b_packs, g_packs, big_packs, spread, pack, square,
    logs_all, chip_logs, chip_decay, own_decay, chip_state,
    state, up_in, first_out, first_in, second_out, second_in, back_out, back_in,
    in_sems, send_sems, halo_recv, log_recv, up_recvs, first_recvs, second_recvs, back_recvs,
):
    place = lax.axis_index("seq")
    chips = count // 2
    owners = chips // 2
    chip, core = place // 2, lax.rem(place, 2)
    lowest = chips // 4
    part = LANES // owners
    half = LANES // 2
    tokens = blocks * GROUP
    tiles = inner // WIDE
    early = updates.shape[0]
    partner = place + 1 - 2 * core

    def peer(step):
        return lax.rem(place + step, count)

    def columns_of(tile):
        if isinstance(tile, int):
            return pl.ds(tile * WIDE, WIDE)
        return pl.ds(pl.multiple_of(tile * WIDE, WIDE), WIDE)

    def send(source, target, send_sem, recv_sem, device):
        return pltpu.make_async_remote_copy(
            src_ref=source, dst_ref=target, send_sem=send_sem, recv_sem=recv_sem,
            device_id={"seq": device}, device_id_type=pl.DeviceIdType.MESH,
        )

    def in_copy(start, width, sem):
        columns = pl.ds(start, width)
        return pltpu.make_async_copy(whole_ref.at[:, columns], inbuf.at[pl.ds(EDGE, tokens), columns], in_sems.at[sem])

    bc_in, x_in = in_copy(inner, WIDE, 0), in_copy(0, inner, 1)

    def y_copy(tile, block):
        columns, span = columns_of(tile), pl.ds(block * GROUP, GROUP)
        return pltpu.make_async_copy(rows_out.at[span, columns], y_ref.at[span, columns], in_sems.at[2])

    halo_copy = send(
        whole_ref.at[pl.ds(tokens - EDGE, EDGE)], inbuf.at[pl.ds(0, EDGE)], send_sems.at[0], halo_recv.at[0], peer(1)
    )

    def log_copy(hop):
        return send(logs_all.at[place], logs_all.at[place], send_sems.at[1], log_recv.at[0], peer(hop))

    everyone = logs_all.at[pl.ds(0, count - 1)]
    all_logs = send(everyone, everyone, send_sems.at[1], log_recv.at[0], partner)

    def turned(high, low):
        square[0:heads] = jnp.broadcast_to(high, (heads, LANES))
        square[half : half + heads] = jnp.broadcast_to(low, (heads, LANES))
        return square[...].T[0:8]

    def column(ref):
        square[0:1, 0:heads] = ref[...].reshape(1, heads)
        return jnp.broadcast_to(square[0:1], (LANES, LANES)).T[0:heads, 0:1]

    barrier = pltpu.get_barrier_semaphore()
    for hop in range(1, count):
        pl.semaphore_signal(barrier, inc=1, device_id={"seq": peer(hop)}, device_id_type=pl.DeviceIdType.MESH)
    bc_in.start()
    x_in.start()
    squares_ref[...] = jnp.zeros_like(squares_ref)
    square[...] = jnp.zeros_like(square)
    pack[...] = jnp.zeros_like(pack)
    step_bias, rate = column(step_bias_ref), column(rate_ref)
    square[...] = jnp.zeros_like(square)
    shifted = raw_ref[...].astype(F32) + step_bias
    step = jnp.maximum(shifted, 0.0) + jnp.log(1.0 + jnp.exp(-jnp.abs(shifted)))
    logs = -rate * step
    total = jnp.sum(logs, axis=1, keepdims=True)
    logs_all[place] = turned(total, jnp.zeros_like(total))
    pl.semaphore_wait(barrier, count - 1)

    @pl.when(place < count - 1)
    def _():
        halo_copy.start()

    for hop in range(1, count):
        log_copy(hop).start()
    fill_spread(spread, heads)
    ones = lower_triangle().astype(F32).T.astype(BF16)
    high, rest = split(logs)
    middle, low = split(rest)
    before = jnp.zeros((heads, 1), F32)
    for block in range(blocks):
        span = slice(block * GROUP, (block + 1) * GROUP)
        cum = dot(high[:, span].astype(BF16), ones) + (
            dot(middle[:, span].astype(BF16), ones) + dot(low[:, span].astype(BF16), ones)
        )
        end = cum[:, GROUP - 1 : GROUP]
        mid = 0.5 * end
        first, second = split(jnp.exp(cum - mid))
        pack[0:heads, :] = first
        pack[half : half + heads, :] = second
        a_packs[span] = pack[...].T.astype(BF16)
        first, second = split(jnp.exp(mid - cum) * step[:, span])
        pack[0:heads, :] = first
        pack[half : half + heads, :] = second
        b_packs[span] = pack[...].T.astype(BF16)
        first, second = split(jnp.exp(mid))
        g_packs[8 * block : 8 * block + 8] = turned(first, second)
        first, second = split(jnp.exp(before + mid))
        big_packs[8 * block : 8 * block + 8] = turned(first, second)
        before = before + end

    def mix(block, tile):
        pieces = []
        top = block * GROUP
        for piece in range(WIDE // LANES):
            if isinstance(tile, int):
                lanes = pl.ds(tile * WIDE + piece * LANES, LANES)
            else:
                lanes = pl.ds(pl.multiple_of(tile * WIDE + piece * LANES, LANES), LANES)
            slot = block * (WIDE // LANES) + piece
            rows = inbuf[top + EDGE : top + EDGE + GROUP, lanes].astype(F32)
            taps[slot, 0:HALO] = inbuf[top : top + EDGE, lanes].astype(F32)[EDGE - HALO :]
            taps[slot, HALO:] = rows
            weights = 0.5 * weight_ref[:, lanes]
            value = rows * weights[3:4] + 0.5 * bias_ref[lanes].reshape(1, LANES)
            for k in range(3):
                value = value + taps[slot, HALO - 3 + k : HALO - 3 + k + GROUP] * weights[k : k + 1]
            pieces.append(value + value * jnp.tanh(value))
        return jnp.concatenate(pieces, axis=1)

    bc_in.wait()

    triangle = lower_triangle()

    def side_block(block):
        span = slice(block * GROUP, (block + 1) * GROUP)
        bc = mix(block, tiles).astype(BF16)
        b, c = bc[:, :LANES], bc[:, LANES:]
        c_rows[span] = c
        turn = b.astype(F32).T.astype(BF16)
        mixer[block, 0:GROUP] = jnp.where(triangle, dot(c, turn), 0.0).astype(BF16)
        mixer[block, GROUP:] = turn

    def front_block(tile, block):
        columns = columns_of(tile)
        span = slice(block * GROUP, (block + 1) * GROUP)
        scaled = (mix(block, tile) * dot(b_packs[span], spread[:, columns])).astype(BF16)
        product = dot(mixer[block], scaled)
        local[span, columns] = product[:GROUP]
        return product[GROUP:]

    def early_body(tile, _):
        for block in range(1, blocks):
            updates[tile, block - 1] = front_block(tile, block)
        return 0

    for block in range(1, blocks):
        side_block(block)
    x_in.wait()
    lax.fori_loop(0, early, early_body, 0)

    @pl.when(place > 0)
    def _():
        halo_copy.wait_recv()

    @pl.when(place == 0)
    def _():
        inbuf[0:EDGE] = jnp.zeros((EDGE, inbuf.shape[1]), BF16)

    @pl.when(chip == 0)
    def _():
        second_in[...] = jnp.zeros_like(second_in)

    side_block(0)

    def front_tile(tile, ready):
        columns = columns_of(tile)
        wide = spread[:, columns]
        g_all = dot(g_packs[...].astype(BF16), wide)
        carried = None
        for block in range(blocks):
            update = updates[tile, block - 1] if ready and block > 0 else front_block(tile, block)
            g = g_all[8 * block : 8 * block + 1]
            if block == 0:
                carried = g * update
            else:
                kept = g * carried
                held[block - 1, :, columns] = kept.astype(BF16)
                carried = g * (kept + update)
        state[tile] = carried

    def back_tile(tile):
        columns = columns_of(tile)
        wide = spread[:, columns]
        big_all = dot(big_packs[...].astype(BF16), wide)
        arrived = back_in[tile]
        for block in range(blocks):
            span = slice(block * GROUP, (block + 1) * GROUP)
            start = big_all[8 * block : 8 * block + 1] * arrived
            if block > 0:
                start = start + held[block - 1, :, columns].astype(F32)
            value = local[span, columns] + dot(c_rows[span], start.astype(BF16))
            y = value * dot(a_packs[span], wide)
            rows_out[span, columns] = y.astype(BF16)
            own = y * y
            own = own[:, :LANES] + own[:, LANES:]
            squares_ref[span] = squares_ref[span] + own
            y_copy(tile, block).start()

    def leads(tile):
        return lax.rem(tile + tiles, 2) == core

    def up_copy(tile):
        return send(state.at[tile], up_in.at[tile], send_sems.at[2], up_recvs.at[tile // 2], partner)

    def back_copy(tile):
        return send(back_out.at[tile], back_in.at[tile], send_sems.at[3], back_recvs.at[tile // 2], partner)

    def first_copy(tile, owner):
        return send(
            first_out.at[tile, owner], first_in.at[tile, chip],
            send_sems.at[4], first_recvs.at[tile // 2], 2 * (lowest + owner) + core,
        )

    def first_arrivals(tile):
        slots = first_in.at[tile, pl.ds(0, chips - 2)]
        return send(slots, slots, send_sems.at[4], first_recvs.at[tile // 2], partner)

    def second_copy(tile, other):
        return send(
            second_out.at[tile, other], second_in.at[tile, chip - lowest],
            send_sems.at[5], second_recvs.at[tile // 2], 2 * other + core,
        )

    def second_arrivals(tile, number):
        slots = second_in.at[tile, pl.ds(0, number)]
        return send(slots, slots, send_sems.at[5], second_recvs.at[tile // 2], partner)

    def rows_of(owner):
        return slice(owner * part, (owner + 1) * part)

    owning = (chip >= lowest) & (chip < lowest + owners)

    def logs_finish():
        all_logs.wait_recv()
        lane = lax.broadcasted_iota(jnp.int32, (8, LANES), 1)

        def packed(log):
            first, second = split(jnp.exp(log))
            return jnp.where(lane < half, first, pltpu.roll(second, half, 1))

        for other in range(chips):
            chip_logs[other : other + 1] = (logs_all[2 * other] + logs_all[2 * other + 1])[0:1]
        chip_pack = jnp.concatenate([packed(chip_logs[row : row + 8]) for row in range(0, chips, 8)], axis=0).astype(BF16)
        own_pack = jnp.concatenate([packed(logs_all[2 * chip]), packed(logs_all[2 * chip + 1])], axis=0).astype(BF16)
        for tile in range(tiles):
            columns = columns_of(tile)
            chip_decay[:, columns] = dot(chip_pack, spread[:, columns])
            own_decay[:, columns] = dot(own_pack, spread[:, columns])

    def pair_start(tile):
        @pl.when(jnp.logical_not(leads(tile)))
        def _():
            up_copy(tile).start()

    def first_step(tile):
        @pl.when(leads(tile))
        def _():
            up_copy(tile).wait_recv()
            got, mine = up_in[tile], state[tile]
            earlier = jnp.where(core == 0, mine, got)
            later = jnp.where(core == 0, got, mine)
            state[tile] = earlier
            chip_state[...] = own_decay[8:16, columns_of(tile)][0:1] * earlier + later
            for owner in range(owners):
                first_out[tile, owner] = chip_state[rows_of(owner)].astype(BF16)

                @pl.when((chip != lowest + owner) & (chip < chips - 1))
                def _():
                    first_copy(tile, owner).start()

                @pl.when(chip == lowest + owner)
                def _():
                    first_in[tile, chip] = first_out[tile, owner]

    def second_step(tile):
        @pl.when(leads(tile) & owning)
        def _():
            first_arrivals(tile).wait_recv()
            prefix = jnp.zeros((part, WIDE), F32)
            decays = chip_decay[:, columns_of(tile)]
            for other in range(chips):
                if other > 0:
                    second_out[tile, other] = prefix.astype(BF16)

                    @pl.when(chip != other)
                    def _():
                        second_copy(tile, other).start()

                    @pl.when(chip == other)
                    def _():
                        second_in[tile, chip - lowest] = second_out[tile, other]

                if other < chips - 1:
                    prefix = decays[other : other + 1] * prefix + first_in[tile, other].astype(F32)

    def third_step(tile):
        @pl.when(leads(tile))
        def _():
            @pl.when(owning)
            def _():
                second_arrivals(tile, owners - 1).wait_recv()

            @pl.when((chip > 0) & jnp.logical_not(owning))
            def _():
                second_arrivals(tile, owners).wait_recv()

            for owner in range(owners):
                chip_state[rows_of(owner)] = second_in[tile, owner].astype(F32)
            earlier = chip_state[...]
            later = own_decay[0:8, columns_of(tile)][0:1] * earlier + state[tile]
            back_out[tile] = jnp.where(core == 0, later, earlier)
            back_copy(tile).start()
            back_in[tile] = jnp.where(core == 0, earlier, later)

    def fourth_step(tile):
        @pl.when(jnp.logical_not(leads(tile)))
        def _():
            back_copy(tile).wait_recv()

    last = tiles - 1

    def early_front_body(tick, _):
        front_tile(tick, True)
        pair_start(tick)

        @pl.when(tick == 1)
        def _():
            logs_finish()

        @pl.when(tick >= 1)
        def _():
            first_step(tick - 1)

        return 0

    def front_body(tick, _):
        front_tile(tick, False)
        pair_start(tick)
        first_step(tick - 1)

        @pl.when(tick >= 5)
        def _():
            second_step(tick - 5)

        @pl.when(tick >= 9)
        def _():
            third_step(tick - 9)

        return 0

    lax.fori_loop(0, early, early_front_body, 0)
    lax.fori_loop(early, tiles, front_body, 0)

    def back_body(tile, _):
        @pl.when(tile == 1)
        def _():
            first_step(last)

        @pl.when(tile + tiles - 5 < last)
        def _():
            second_step(tile + tiles - 5)

        @pl.when(tile == tiles // 2)
        def _():
            second_step(last)

        @pl.when(tile + tiles - 9 < last)
        def _():
            third_step(tile + tiles - 9)

        @pl.when(tile == last)
        def _():
            third_step(last)

        fourth_step(tile)
        back_tile(tile)
        return 0

    lax.fori_loop(0, tiles, back_body, 0)
    squares_copy = pltpu.make_async_copy(squares_ref, squares_out, in_sems.at[3])
    squares_copy.start()

    @pl.when(place < count - 1)
    def _():
        halo_copy.wait_send()

    all_logs.wait_send()
    led = tiles // 2

    def sent(ref, sem):
        send(ref, ref, sem, up_recvs.at[0], partner).wait_send()

    sent(state.at[pl.ds(0, led)], send_sems.at[2])
    sent(back_out.at[pl.ds(0, led)], send_sems.at[3])

    @pl.when(owning)
    def _():
        sent(first_out.at[pl.ds(0, led), pl.ds(0, owners - 1)], send_sems.at[4])
        sent(second_out.at[pl.ds(0, led), pl.ds(0, chips - 2)], send_sems.at[5])

    @pl.when(jnp.logical_not(owning) & (chip < chips - 1))
    def _():
        sent(first_out.at[pl.ds(0, led)], send_sems.at[4])

    pltpu.make_async_copy(rows_out, y_ref, in_sems.at[2]).wait()
    squares_copy.wait()


def back_kernel(inner, y_ref, squares_ref, gain_ref, out_ref):
    mean = jnp.sum(squares_ref[...], axis=1, keepdims=True) * (1.0 / inner)
    scale = lax.rsqrt(mean + 1e-05)
    for start in range(0, inner, LANES):
        columns = slice(start, start + LANES)
        out_ref[:, columns] = (y_ref[:, columns].astype(F32) * scale * gain_ref[columns].reshape(1, LANES)).astype(BF16)


def per_device(conv_input, step_raw, conv_weight, conv_bias, step_bias, decay_rate, norm_gain):
    tokens, conv_dim = conv_input.shape
    heads, inner = decay_rate.shape[0], norm_gain.shape[0]
    blocks, tiles = tokens // GROUP, inner // WIDE
    count = lax.axis_size("seq")
    chips = count // 2
    owners = chips // 2
    part = LANES // owners

    def vmem(*shape, dtype=BF16):
        return pltpu.VMEM(shape, dtype)

    shape = jax.ShapeDtypeStruct
    inside, anywhere = pl.BlockSpec(memory_space=pltpu.VMEM), pl.BlockSpec(memory_space=pl.ANY)
    dma = pltpu.SemaphoreType.DMA
    y, squares = pl.pallas_call(
        functools.partial(front_kernel, inner, heads, blocks, count),
        in_specs=[anywhere] + [inside] * 5,
        out_specs=[anywhere, anywhere],
        out_shape=[shape((tokens, inner), BF16), shape((tokens, LANES), F32)],
        scratch_shapes=[
            vmem(tokens, LANES, dtype=F32), vmem(EDGE + tokens, conv_dim), vmem(blocks * WIDE // LANES, HALO + GROUP, LANES, dtype=F32), vmem(tokens, inner, dtype=F32),
            vmem(EARLY, blocks - 1, LANES, WIDE, dtype=F32), vmem(tokens, inner), vmem(blocks - 1, LANES, inner),
            vmem(blocks, GROUP + LANES, GROUP), vmem(tokens, LANES), vmem(tokens, LANES),
            vmem(tokens, LANES), vmem(8 * blocks, LANES, dtype=F32), vmem(8 * blocks, LANES, dtype=F32),
            vmem(LANES, inner), vmem(LANES, GROUP, dtype=F32), vmem(LANES, LANES, dtype=F32),
            vmem(count, 8, LANES, dtype=F32), vmem(chips, LANES, dtype=F32), vmem(chips, inner, dtype=F32),
            vmem(16, inner, dtype=F32), vmem(LANES, WIDE, dtype=F32),
            vmem(tiles, LANES, WIDE, dtype=F32), vmem(tiles, LANES, WIDE, dtype=F32),
            vmem(tiles, owners, part, WIDE), vmem(tiles, chips, part, WIDE),
            vmem(tiles, chips, part, WIDE), vmem(tiles, owners, part, WIDE),
            vmem(tiles, LANES, WIDE, dtype=F32), vmem(tiles, LANES, WIDE, dtype=F32),
            dma((4,)), dma((6,)), dma((1,)), dma((1,)), dma((tiles // 2,)), dma((tiles // 2,)), dma((tiles // 2,)), dma((tiles // 2,)),
        ],
        compiler_params=pltpu.CompilerParams(collective_id=0, has_side_effects=True, vmem_limit_bytes=60 * 1024 * 1024),
        name="front",
    )(conv_input, step_raw.T, conv_weight, conv_bias, step_bias, decay_rate)
    rows = 2 * GROUP
    return pl.pallas_call(
        functools.partial(back_kernel, inner),
        grid=(tokens // rows,),
        in_specs=[
            pl.BlockSpec((rows, inner), lambda i: (i, 0)), pl.BlockSpec((rows, LANES), lambda i: (i, 0)),
            pl.BlockSpec((inner,), lambda i: (0,)),
        ],
        out_specs=pl.BlockSpec((rows, inner), lambda i: (i, 0)),
        out_shape=shape((tokens, inner), BF16),
        name="back",
    )(y, squares, norm_gain)


def solution(mesh):
    placed = (P(("parts", "seq"), None), P(("parts", "seq"), None), P(), P(), P(), P(), P())
    return jax.shard_map(
        per_device, mesh=mesh, in_specs=placed, out_specs=P(("parts", "seq"), None), check_vma=False
    )
```

```python
import functools

import jax
import jax.numpy as jnp
from jax import lax
from jax.experimental import pallas as pl
from jax.experimental.pallas import tpu as pltpu
from jax.sharding import PartitionSpec as P

GROUP = 256
WIDE = 256
LANES = 128
HALO = 8
EDGE = 16
EARLY = 3
F32, BF16 = jnp.float32, jnp.bfloat16


def dot(left, right):
    return jnp.dot(left, right, preferred_element_type=F32)


def split(value):
    high = value.astype(BF16).astype(F32)
    return high, value - high


def lower_triangle():
    rows = lax.broadcasted_iota(jnp.int32, (GROUP, GROUP), 0)
    columns = lax.broadcasted_iota(jnp.int32, (GROUP, GROUP), 1)
    return rows >= columns


def fill_spread(spread, heads):
    width = spread.shape[1] // heads
    rows = lax.broadcasted_iota(jnp.int32, spread.shape, 0)
    columns = lax.broadcasted_iota(jnp.int32, spread.shape, 1)
    rows = jnp.where(rows >= LANES // 2, rows - LANES // 2, rows)
    start = rows * width
    spread[...] = jnp.where((columns >= start) & (columns < start + width), 1.0, 0.0).astype(BF16)


def front_kernel(
    inner, heads, blocks, count,
    whole_ref, raw_ref, weight_ref, bias_ref, step_bias_ref, rate_ref,
    y_ref, squares_out,
    squares_ref, inbuf, taps, local, updates, rows_out, held, mixer, c_rows, a_packs, b_packs, g_packs, big_packs, spread, pack, square,
    logs_all, chip_logs, chip_decay, own_decay, chip_state,
    state, up_in, first_out, first_in, second_out, second_in, back_out, back_in,
    in_sems, send_sems, halo_recv, log_recv, up_recvs, first_recvs, second_recvs, back_recvs,
):
    place = lax.axis_index("seq")
    chips = count // 2
    owners = chips // 2
    chip, core = place // 2, lax.rem(place, 2)
    lowest = chips // 4
    part = LANES // owners
    half = LANES // 2
    tokens = blocks * GROUP
    tiles = inner // WIDE
    early = updates.shape[0]
    partner = place + 1 - 2 * core

    def peer(step):
        return lax.rem(place + step, count)

    def columns_of(tile):
        if isinstance(tile, int):
            return pl.ds(tile * WIDE, WIDE)
        return pl.ds(pl.multiple_of(tile * WIDE, WIDE), WIDE)

    def send(source, target, send_sem, recv_sem, device):
        return pltpu.make_async_remote_copy(
            src_ref=source, dst_ref=target, send_sem=send_sem, recv_sem=recv_sem,
            device_id={"seq": device}, device_id_type=pl.DeviceIdType.MESH,
        )

    def in_copy(start, width, sem):
        columns = pl.ds(start, width)
        return pltpu.make_async_copy(whole_ref.at[:, columns], inbuf.at[pl.ds(EDGE, tokens), columns], in_sems.at[sem])

    ahead = early * WIDE
    bc_in, x_in, rest_in = in_copy(inner, WIDE, 0), in_copy(0, ahead, 1), in_copy(ahead, inner - ahead, 4)

    def y_copy(tile, block):
        columns, span = columns_of(tile), pl.ds(block * GROUP, GROUP)
        return pltpu.make_async_copy(rows_out.at[span, columns], y_ref.at[span, columns], in_sems.at[2])

    halo_copy = send(
        whole_ref.at[pl.ds(tokens - EDGE, EDGE)], inbuf.at[pl.ds(0, EDGE)], send_sems.at[0], halo_recv.at[0], peer(1)
    )

    def log_copy(hop):
        return send(logs_all.at[place], logs_all.at[place], send_sems.at[1], log_recv.at[0], peer(hop))

    everyone = logs_all.at[pl.ds(0, count - 1)]
    all_logs = send(everyone, everyone, send_sems.at[1], log_recv.at[0], partner)

    def turned(high, low):
        square[0:heads] = jnp.broadcast_to(high, (heads, LANES))
        square[half : half + heads] = jnp.broadcast_to(low, (heads, LANES))
        return square[...].T[0:8]

    def column(ref):
        square[0:1, 0:heads] = ref[...].reshape(1, heads)
        return jnp.broadcast_to(square[0:1], (LANES, LANES)).T[0:heads, 0:1]

    barrier = pltpu.get_barrier_semaphore()
    for hop in range(1, count):
        pl.semaphore_signal(barrier, inc=1, device_id={"seq": peer(hop)}, device_id_type=pl.DeviceIdType.MESH)
    bc_in.start()
    x_in.start()
    rest_in.start()
    squares_ref[...] = jnp.zeros_like(squares_ref)
    square[...] = jnp.zeros_like(square)
    pack[...] = jnp.zeros_like(pack)
    step_bias, rate = column(step_bias_ref), column(rate_ref)
    square[...] = jnp.zeros_like(square)
    shifted = raw_ref[...].astype(F32) + step_bias
    step = jnp.maximum(shifted, 0.0) + jnp.log(1.0 + jnp.exp(-jnp.abs(shifted)))
    logs = -rate * step
    total = jnp.sum(logs, axis=1, keepdims=True)
    logs_all[place] = turned(total, jnp.zeros_like(total))
    pl.semaphore_wait(barrier, count - 1)

    @pl.when(place < count - 1)
    def _():
        halo_copy.start()

    for hop in range(1, count):
        log_copy(hop).start()
    fill_spread(spread, heads)
    ones = lower_triangle().astype(F32).T.astype(BF16)
    high, rest = split(logs)
    middle, low = split(rest)
    before = jnp.zeros((heads, 1), F32)
    for block in range(blocks):
        span = slice(block * GROUP, (block + 1) * GROUP)
        cum = dot(high[:, span].astype(BF16), ones) + (
            dot(middle[:, span].astype(BF16), ones) + dot(low[:, span].astype(BF16), ones)
        )
        end = cum[:, GROUP - 1 : GROUP]
        mid = 0.5 * end
        first, second = split(jnp.exp(cum - mid))
        pack[0:heads, :] = first
        pack[half : half + heads, :] = second
        a_packs[span] = pack[...].T.astype(BF16)
        first, second = split(jnp.exp(mid - cum) * step[:, span])
        pack[0:heads, :] = first
        pack[half : half + heads, :] = second
        b_packs[span] = pack[...].T.astype(BF16)
        first, second = split(jnp.exp(mid))
        g_packs[8 * block : 8 * block + 8] = turned(first, second)
        first, second = split(jnp.exp(before + mid))
        big_packs[8 * block : 8 * block + 8] = turned(first, second)
        before = before + end

    def mix(block, tile):
        pieces = []
        top = block * GROUP
        for piece in range(WIDE // LANES):
            if isinstance(tile, int):
                lanes = pl.ds(tile * WIDE + piece * LANES, LANES)
            else:
                lanes = pl.ds(pl.multiple_of(tile * WIDE + piece * LANES, LANES), LANES)
            slot = block * (WIDE // LANES) + piece
            rows = inbuf[top + EDGE : top + EDGE + GROUP, lanes].astype(F32)
            taps[slot, 0:HALO] = inbuf[top : top + EDGE, lanes].astype(F32)[EDGE - HALO :]
            taps[slot, HALO:] = rows
            weights = 0.5 * weight_ref[:, lanes]
            value = rows * weights[3:4] + 0.5 * bias_ref[lanes].reshape(1, LANES)
            for k in range(3):
                value = value + taps[slot, HALO - 3 + k : HALO - 3 + k + GROUP] * weights[k : k + 1]
            pieces.append(value + value * jnp.tanh(value))
        return jnp.concatenate(pieces, axis=1)

    bc_in.wait()

    triangle = lower_triangle()

    def side_block(block):
        span = slice(block * GROUP, (block + 1) * GROUP)
        bc = mix(block, tiles).astype(BF16)
        b, c = bc[:, :LANES], bc[:, LANES:]
        c_rows[span] = c
        turn = b.astype(F32).T.astype(BF16)
        mixer[block, 0:GROUP] = jnp.where(triangle, dot(c, turn), 0.0).astype(BF16)
        mixer[block, GROUP:] = turn

    def front_block(tile, block):
        columns = columns_of(tile)
        span = slice(block * GROUP, (block + 1) * GROUP)
        scaled = (mix(block, tile) * dot(b_packs[span], spread[:, columns])).astype(BF16)
        product = dot(mixer[block], scaled)
        local[span, columns] = product[:GROUP]
        return product[GROUP:]

    def early_body(tile, _):
        for block in range(1, blocks):
            updates[tile, block - 1] = front_block(tile, block)
        return 0

    @pl.when(chip == 0)
    def _():
        second_in[...] = jnp.zeros_like(second_in)

    for block in range(1, blocks):
        side_block(block)
    x_in.wait()
    lax.fori_loop(0, early, early_body, 0)

    @pl.when(place > 0)
    def _():
        halo_copy.wait_recv()

    @pl.when(place == 0)
    def _():
        inbuf[0:EDGE] = jnp.zeros((EDGE, inbuf.shape[1]), BF16)

    side_block(0)

    def front_tile(tile, ready):
        columns = columns_of(tile)
        wide = spread[:, columns]
        g_all = dot(g_packs[...].astype(BF16), wide)
        carried = None
        for block in range(blocks):
            update = updates[tile, block - 1] if ready and block > 0 else front_block(tile, block)
            g = g_all[8 * block : 8 * block + 1]
            if block == 0:
                carried = g * update
            else:
                kept = g * carried
                held[block - 1, :, columns] = kept.astype(BF16)
                carried = g * (kept + update)
        state[tile] = carried

    def back_tile(tile):
        columns = columns_of(tile)
        wide = spread[:, columns]
        big_all = dot(big_packs[...].astype(BF16), wide)
        arrived = back_in[tile]
        for block in range(blocks):
            span = slice(block * GROUP, (block + 1) * GROUP)
            start = big_all[8 * block : 8 * block + 1] * arrived
            if block > 0:
                start = start + held[block - 1, :, columns].astype(F32)
            value = local[span, columns] + dot(c_rows[span], start.astype(BF16))
            y = value * dot(a_packs[span], wide)
            rows_out[span, columns] = y.astype(BF16)
            own = y * y
            own = own[:, :LANES] + own[:, LANES:]
            squares_ref[span] = squares_ref[span] + own
            y_copy(tile, block).start()

    def leads(tile):
        return lax.rem(tile + tiles, 2) == core

    def up_copy(tile):
        return send(state.at[tile], up_in.at[tile], send_sems.at[2], up_recvs.at[tile // 2], partner)

    def back_copy(tile):
        return send(back_out.at[tile], back_in.at[tile], send_sems.at[3], back_recvs.at[tile // 2], partner)

    def first_copy(tile, owner):
        return send(
            first_out.at[tile, owner], first_in.at[tile, chip],
            send_sems.at[4], first_recvs.at[tile // 2], 2 * (lowest + owner) + core,
        )

    def first_arrivals(tile):
        slots = first_in.at[tile, pl.ds(0, chips - 2)]
        return send(slots, slots, send_sems.at[4], first_recvs.at[tile // 2], partner)

    def second_copy(tile, other):
        return send(
            second_out.at[tile, other], second_in.at[tile, chip - lowest],
            send_sems.at[5], second_recvs.at[tile // 2], 2 * other + core,
        )

    def second_arrivals(tile, number):
        slots = second_in.at[tile, pl.ds(0, number)]
        return send(slots, slots, send_sems.at[5], second_recvs.at[tile // 2], partner)

    def rows_of(owner):
        return slice(owner * part, (owner + 1) * part)

    owning = (chip >= lowest) & (chip < lowest + owners)

    def logs_finish():
        all_logs.wait_recv()
        lane = lax.broadcasted_iota(jnp.int32, (8, LANES), 1)

        def packed(log):
            first, second = split(jnp.exp(log))
            return jnp.where(lane < half, first, pltpu.roll(second, half, 1))

        for other in range(chips):
            chip_logs[other : other + 1] = (logs_all[2 * other] + logs_all[2 * other + 1])[0:1]
        chip_pack = jnp.concatenate([packed(chip_logs[row : row + 8]) for row in range(0, chips, 8)], axis=0).astype(BF16)
        own_pack = jnp.concatenate([packed(logs_all[2 * chip]), packed(logs_all[2 * chip + 1])], axis=0).astype(BF16)
        for tile in range(tiles):
            columns = columns_of(tile)
            chip_decay[:, columns] = dot(chip_pack, spread[:, columns])
            own_decay[:, columns] = dot(own_pack, spread[:, columns])

    def pair_start(tile):
        @pl.when(jnp.logical_not(leads(tile)))
        def _():
            up_copy(tile).start()

    def first_step(tile):
        @pl.when(leads(tile))
        def _():
            up_copy(tile).wait_recv()
            got, mine = up_in[tile], state[tile]
            earlier = jnp.where(core == 0, mine, got)
            later = jnp.where(core == 0, got, mine)
            state[tile] = earlier
            chip_state[...] = own_decay[8:16, columns_of(tile)][0:1] * earlier + later
            for owner in range(owners):
                first_out[tile, owner] = chip_state[rows_of(owner)].astype(BF16)

                @pl.when((chip != lowest + owner) & (chip < chips - 1))
                def _():
                    first_copy(tile, owner).start()

                @pl.when(chip == lowest + owner)
                def _():
                    first_in[tile, chip] = first_out[tile, owner]

    def second_step(tile):
        @pl.when(leads(tile) & owning)
        def _():
            first_arrivals(tile).wait_recv()
            prefix = jnp.zeros((part, WIDE), F32)
            decays = chip_decay[:, columns_of(tile)]
            for other in range(chips):
                if other > 0:
                    second_out[tile, other] = prefix.astype(BF16)

                    @pl.when(chip != other)
                    def _():
                        second_copy(tile, other).start()

                    @pl.when(chip == other)
                    def _():
                        second_in[tile, chip - lowest] = second_out[tile, other]

                if other < chips - 1:
                    prefix = decays[other : other + 1] * prefix + first_in[tile, other].astype(F32)

    def third_step(tile):
        @pl.when(leads(tile))
        def _():
            @pl.when(owning)
            def _():
                second_arrivals(tile, owners - 1).wait_recv()

            @pl.when((chip > 0) & jnp.logical_not(owning))
            def _():
                second_arrivals(tile, owners).wait_recv()

            for owner in range(owners):
                chip_state[rows_of(owner)] = second_in[tile, owner].astype(F32)
            earlier = chip_state[...]
            later = own_decay[0:8, columns_of(tile)][0:1] * earlier + state[tile]
            back_out[tile] = jnp.where(core == 0, later, earlier)
            back_copy(tile).start()
            back_in[tile] = jnp.where(core == 0, earlier, later)

    def fourth_step(tile):
        @pl.when(jnp.logical_not(leads(tile)))
        def _():
            back_copy(tile).wait_recv()

    last = tiles - 1

    def early_front_body(tick, _):
        front_tile(tick, True)
        pair_start(tick)

        @pl.when(tick == 1)
        def _():
            logs_finish()

        @pl.when(tick >= 1)
        def _():
            first_step(tick - 1)

        return 0

    def front_body(tick, _):
        front_tile(tick, False)
        pair_start(tick)
        first_step(tick - 1)

        @pl.when(tick >= 5)
        def _():
            second_step(tick - 5)

        @pl.when(tick >= 9)
        def _():
            third_step(tick - 9)

        return 0

    lax.fori_loop(0, early, early_front_body, 0)
    rest_in.wait()
    lax.fori_loop(early, tiles, front_body, 0)

    def back_body(tile, _):
        @pl.when(tile == 1)
        def _():
            first_step(last)

        @pl.when(tile + tiles - 5 < last)
        def _():
            second_step(tile + tiles - 5)

        @pl.when(tile == tiles // 2)
        def _():
            second_step(last)

        @pl.when(tile + tiles - 9 < last)
        def _():
            third_step(tile + tiles - 9)

        @pl.when(tile == last)
        def _():
            third_step(last)

        fourth_step(tile)
        back_tile(tile)
        return 0

    lax.fori_loop(0, tiles, back_body, 0)
    squares_copy = pltpu.make_async_copy(squares_ref, squares_out, in_sems.at[3])
    squares_copy.start()

    @pl.when(place < count - 1)
    def _():
        halo_copy.wait_send()

    all_logs.wait_send()
    led = tiles // 2

    def sent(ref, sem):
        send(ref, ref, sem, up_recvs.at[0], partner).wait_send()

    sent(state.at[pl.ds(0, led)], send_sems.at[2])
    sent(back_out.at[pl.ds(0, led)], send_sems.at[3])

    @pl.when(owning)
    def _():
        sent(first_out.at[pl.ds(0, led), pl.ds(0, owners - 1)], send_sems.at[4])
        sent(second_out.at[pl.ds(0, led), pl.ds(0, chips - 2)], send_sems.at[5])

    @pl.when(jnp.logical_not(owning) & (chip < chips - 1))
    def _():
        sent(first_out.at[pl.ds(0, led)], send_sems.at[4])

    pltpu.make_async_copy(rows_out, y_ref, in_sems.at[2]).wait()
    squares_copy.wait()


def back_kernel(inner, y_ref, squares_ref, gain_ref, out_ref):
    mean = jnp.sum(squares_ref[...], axis=1, keepdims=True) * (1.0 / inner)
    scale = lax.rsqrt(mean + 1e-05)
    for start in range(0, inner, LANES):
        columns = slice(start, start + LANES)
        out_ref[:, columns] = (y_ref[:, columns].astype(F32) * scale * gain_ref[columns].reshape(1, LANES)).astype(BF16)


def per_device(conv_input, step_raw, conv_weight, conv_bias, step_bias, decay_rate, norm_gain):
    tokens, conv_dim = conv_input.shape
    heads, inner = decay_rate.shape[0], norm_gain.shape[0]
    blocks, tiles = tokens // GROUP, inner // WIDE
    count = lax.axis_size("seq")
    chips = count // 2
    owners = chips // 2
    part = LANES // owners

    def vmem(*shape, dtype=BF16):
        return pltpu.VMEM(shape, dtype)

    shape = jax.ShapeDtypeStruct
    inside, anywhere = pl.BlockSpec(memory_space=pltpu.VMEM), pl.BlockSpec(memory_space=pl.ANY)
    dma = pltpu.SemaphoreType.DMA
    y, squares = pl.pallas_call(
        functools.partial(front_kernel, inner, heads, blocks, count),
        in_specs=[anywhere] + [inside] * 5,
        out_specs=[anywhere, anywhere],
        out_shape=[shape((tokens, inner), BF16), shape((tokens, LANES), F32)],
        scratch_shapes=[
            vmem(tokens, LANES, dtype=F32), vmem(EDGE + tokens, conv_dim), vmem(blocks * WIDE // LANES, HALO + GROUP, LANES, dtype=F32), vmem(tokens, inner, dtype=F32),
            vmem(EARLY, blocks - 1, LANES, WIDE, dtype=F32), vmem(tokens, inner), vmem(blocks - 1, LANES, inner),
            vmem(blocks, GROUP + LANES, GROUP), vmem(tokens, LANES), vmem(tokens, LANES),
            vmem(tokens, LANES), vmem(8 * blocks, LANES, dtype=F32), vmem(8 * blocks, LANES, dtype=F32),
            vmem(LANES, inner), vmem(LANES, GROUP, dtype=F32), vmem(LANES, LANES, dtype=F32),
            vmem(count, 8, LANES, dtype=F32), vmem(chips, LANES, dtype=F32), vmem(chips, inner, dtype=F32),
            vmem(16, inner, dtype=F32), vmem(LANES, WIDE, dtype=F32),
            vmem(tiles, LANES, WIDE, dtype=F32), vmem(tiles, LANES, WIDE, dtype=F32),
            vmem(tiles, owners, part, WIDE), vmem(tiles, chips, part, WIDE),
            vmem(tiles, chips, part, WIDE), vmem(tiles, owners, part, WIDE),
            vmem(tiles, LANES, WIDE, dtype=F32), vmem(tiles, LANES, WIDE, dtype=F32),
            dma((5,)), dma((6,)), dma((1,)), dma((1,)), dma((tiles // 2,)), dma((tiles // 2,)), dma((tiles // 2,)), dma((tiles // 2,)),
        ],
        compiler_params=pltpu.CompilerParams(collective_id=0, has_side_effects=True, vmem_limit_bytes=60 * 1024 * 1024),
        name="front",
    )(conv_input, step_raw.T, conv_weight, conv_bias, step_bias, decay_rate)
    rows = 2 * GROUP
    return pl.pallas_call(
        functools.partial(back_kernel, inner),
        grid=(tokens // rows,),
        in_specs=[
            pl.BlockSpec((rows, inner), lambda i: (i, 0)), pl.BlockSpec((rows, LANES), lambda i: (i, 0)),
            pl.BlockSpec((inner,), lambda i: (0,)),
        ],
        out_specs=pl.BlockSpec((rows, inner), lambda i: (i, 0)),
        out_shape=shape((tokens, inner), BF16),
        name="back",
    )(y, squares, norm_gain)


def solution(mesh):
    placed = (P(("parts", "seq"), None), P(("parts", "seq"), None), P(), P(), P(), P(), P())
    return jax.shard_map(
        per_device, mesh=mesh, in_specs=placed, out_specs=P(("parts", "seq"), None), check_vma=False
    )
```
